256 devices in a mesh: tm: 64 (over z, y, core), grp: 4 (over x).
Axes of the slice: x: 4, y: 4, z: 8, core: 2. Of those that a mesh axis runs over, the one named last changes fastest.
Arguments:
- voltages: bfloat16 [1, 24, 2, 2, 262144], P(None, None, None, None, ('tm', 'grp')), may hold values from -8 to 8
- chirp_phase: float32 [24, 512, 512], P(None, 'tm'), may hold values from -3.140625 to 3.140625
- intersection: int32 [24], replicated, may hold values from 1 to 131072
- group_of: int32 [24], replicated, may hold values from 0 to 3, as said below
Outputs:
- group_power: float32 [1, 4, 131072], P(None, None, ('tm', 'grp'))
The draws below stay inside these ranges and needn't reach their ends.
Inputs may be any that keep to these rules, and one draw needn't show every extreme that they name: `group_of`: every one of the 4 groups holds at least one channel and at most 12; some group holds exactly 12.
All inputs are finite; a program needn't handle non-finite values.
Results may differ from the reference program's by a relative error of at most 0.0003.
Values may be sent and summed in bfloat16 or wider, within the bound.
No kernel may reach another device: no remote copies, remote signals or barrier semaphores. Data moves between devices by JAX's collectives and lax.ppermute only.
A program may use at most 128 MiB of HBM per device.

```python
import math
import jax
import jax.numpy as jnp
from jax import lax

BEAMS = 1
POLS = 2
CHANS = 24
NFFT = 262144
F1 = 512
CMAX = 12
F2 = 512
GROUPS = 4
TOUT = 131072


def draw_group_of(key, part):
    seeded = jax.random.fold_in(key, 17)
    pick_key, label_key, shuffle_key = jax.random.split(seeded, 3)
    largest = jax.random.randint(pick_key, (), 0, GROUPS)
    offsets = jax.random.randint(label_key, (CHANS,), 0, GROUPS - 1)
    places = jnp.arange(CHANS, dtype=jnp.int32)
    spread_label = (largest + 1 + offsets) % GROUPS
    forced_label = (largest + 1 + places - CMAX) % GROUPS
    labels = jnp.where(places < CMAX, largest, jnp.where(places < CMAX + GROUPS - 1, forced_label, spread_label))
    shuffle = jax.random.permutation(shuffle_key, CHANS)
    return labels[shuffle].astype(jnp.int32)


def place_ends(entries, key, least, top_value):
    extent = entries.shape
    spot = [jax.random.randint(jax.random.fold_in(key, axis), (), 0, extent[axis]) for axis in range(len(extent))]
    entries = entries.at[tuple(spot)].set(least)
    longest = extent.index(max(extent))
    spot[longest] = (spot[longest] + 1) % extent[longest]
    return entries.at[tuple(spot)].set(top_value)


def shard_levels(key, extent, pieces, low, high):
    gain, own = 1.0, jax.random.fold_in(key, 6)
    for position, parts in pieces:
        draws = jnp.exp(jax.random.uniform(jax.random.fold_in(own, position), (parts,), jnp.float32, low / len(pieces), high / len(pieces)))
        gain = gain * jnp.repeat(draws, extent[position] // parts).reshape([-1 if axis == position else 1 for axis in range(len(extent))])
    return gain


def gaussian(rng, dims, scale, limit, pieces=(), kind=jnp.bfloat16):
    level = shard_levels(rng, dims, pieces, -0.22, 0.18) if pieces else 1.0
    drawn = jax.random.normal(rng, dims, jnp.float32) * scale * level
    return jnp.minimum(jnp.maximum(drawn, -limit), limit).astype(kind)


def setup_inputs(seed: int = 0) -> dict:
    splits = jax.random.split(jax.random.key(seed), 5)
    return {
        "voltages": gaussian(splits[0], (BEAMS, CHANS, POLS, 2, NFFT), 1.0, 8.0, ((4, 256),)),
        "chirp_phase": jnp.clip(jax.random.uniform(splits[1], (CHANS, F1, F2), jnp.float32, -3.140625, 3.140625), -3.140625, 3.140625),
        "intersection": place_ends(jax.random.randint(splits[2], (CHANS,), 1, NFFT // 2 + 1), jax.random.fold_in(splits[2], 1), 1, (NFFT // 2 + 1) - 1).astype(jnp.int32),
        "group_of": draw_group_of(jax.random.fold_in(splits[4], 71), 0),
    }


full_turn = 2.0 * math.pi


def channel_power(samples, phase_table, shift_count):
    values = samples.astype(jnp.float32)
    complex_signal = values[:, :, 0, :] + 1j * values[:, :, 1, :]
    spectrum = jnp.fft.fft(complex_signal, axis=-1)
    bins = jnp.arange(NFFT, dtype=jnp.int32)
    low_bin = bins % F1
    high_bin = bins // F1
    ramp = (low_bin * shift_count + F1 * ((high_bin * shift_count) % F2)) % NFFT
    phase_total = jnp.transpose(phase_table).reshape(NFFT) + full_turn * ramp.astype(jnp.float32) / NFFT
    result = jnp.fft.ifft(spectrum * jnp.exp(1j * phase_total), axis=-1)[:, :, :TOUT]
    return jnp.sum(jnp.real(result) ** 2 + jnp.imag(result) ** 2, axis=1)


def reference(voltages, chirp_phase, intersection, group_of):
    powers = lax.map(lambda items: channel_power(items[0], items[1], items[2]),
                     (jnp.moveaxis(voltages, 1, 0), chirp_phase, intersection))
    member = (group_of[None, :] == jnp.arange(GROUPS, dtype=jnp.int32)[:, None]).astype(jnp.float32)
    counts = jnp.sum(member, axis=1)
    totals = jnp.einsum("gc,cbt->bgt", member, powers, precision=lax.Precision.HIGHEST)
    return totals / (2.0 * counts)[None, :, None]
```

```python
import functools
import math

import jax
import jax.numpy as jnp
import numpy as np
from jax import lax
from jax.experimental import pallas as pl
from jax.experimental.pallas import tpu as pltpu
from jax.sharding import Mesh
from jax.sharding import PartitionSpec as P

NFFT = 262144
F1 = 512
F2 = 512
CHANS = 24
POLS = 2
SERIES = CHANS * POLS
SLOTS = 64
GROUPS = 4
AXES = ("z", "y", "core", "xh", "xl")
SPREAD = ("z", "y", "xh")
SWAP = [(0, 1), (1, 0)]
MIB = 1 << 20

f32 = jnp.float32
bf16 = jnp.bfloat16
i32 = jnp.int32


def cos_sin(index, period):
    angle = 2.0 * np.pi * (index % period) / period
    return np.cos(angle).astype(np.float32), np.sin(angle).astype(np.float32)


@functools.cache
def table_factors():
    m = np.arange(64)
    fine = 16 * (m // 2) + 4 * (m % 2)
    beta = np.arange(8)
    coarse = 8 * (beta // 4) + 2 * (beta // 2 % 2) + beta % 2
    order = (coarse[:, None] + fine[None, :]).reshape(-1)
    column = np.arange(512)
    pairs = []
    for rows_fine, rows_coarse, columns, period in (
        (fine, coarse, order, F1),
        (m, 64 * beta, column, F2),
        (m, 64 * beta, order, F1),
        (fine, coarse, column, NFFT),
    ):
        pairs.append(
            (
                cos_sin(rows_fine[:, None] * columns[None, :], period),
                cos_sin(rows_coarse[:, None] * columns[None, :], period),
            )
        )
    fine_table = np.stack([part for pair in pairs for part in pair[0]])
    coarse_table = np.stack([part for pair in pairs for part in pair[1]])
    return fine_table, coarse_table


def split(value):
    high = value.astype(bf16)
    return high, (value - high.astype(f32)).astype(bf16)


def pack_kernel(v_ref, c_ref, out_ref, wide, narrow, tall):
    x_pos = 2 * lax.axis_index("xh") + lax.axis_index("xl")
    samples = v_ref[...].reshape(SERIES * 2, 1024).astype(f32)
    for i in range(8):
        wide[pl.ds(SERIES * 2 * i, SERIES * 2), :] = samples[:, 128 * i : 128 * i + 128]
    for kk in range(4):
        narrow[pl.ds(CHANS * 8 * kk, CHANS * 8), :] = c_ref[:, pl.ds(128 * kk, 128)]
    for reim in range(2):
        for i in range(8):
            piece = wide[pl.ds(SERIES * 2 * i + reim, SERIES, stride=2), :]
            tall[pl.ds(reim * 8 + i, SERIES, stride=32), :] = piece
    for r in range(2):
        for kk in range(4):
            phase = narrow[pl.ds(CHANS * 8 * kk + 2 * x_pos + r, CHANS, stride=8), :]
            high = phase.astype(bf16).astype(f32)
            low = phase - high
            for pol in range(2):
                base = pol * 32 + 16 + r * 4 + kk
                tall[pl.ds(base, CHANS, stride=64), :] = high
                tall[pl.ds(base + 8, CHANS, stride=64), :] = low
    packed = tall[...].astype(bf16).reshape(SERIES, 32, 128)
    out_ref[pl.ds(0, SERIES)] = packed
    out_ref[pl.ds(SERIES, SLOTS - SERIES)] = packed[: SLOTS - SERIES]


def pack(voltages, chirp):
    return pl.pallas_call(
        pack_kernel,
        out_shape=jax.ShapeDtypeStruct((SLOTS, 32, 128), bf16),
        scratch_shapes=[pltpu.VMEM((SERIES * 16, 128), f32), pltpu.VMEM((CHANS * 32, 128), f32), pltpu.VMEM((SERIES * 32, 128), f32)],
        compiler_params=pltpu.CompilerParams(vmem_limit_bytes=16 * MIB),
        name="pack",
    )(voltages.reshape(CHANS, POLS, 2, 1024), chirp.reshape(CHANS * 8, 512))


def unpack_kernel(got_ref, x_ref, phase_ref, tall):
    tall[...] = got_ref[...].reshape(SLOTS * 32, 128).astype(f32)
    for reim in range(2):
        for i in range(8):
            rows = tall[pl.ds(reim * 8 + i, SLOTS, stride=32), :]
            x_ref[reim, pl.ds(64 * (i // 4), 64), pl.ds(128 * (i % 4), 128)] = rows.astype(bf16)
    scale = 65536.0 / (2.0 * math.pi)
    for r in range(2):
        for kk in range(4):
            high = tall[pl.ds(16 + r * 4 + kk, SLOTS, stride=32), :]
            low = tall[pl.ds(24 + r * 4 + kk, SLOTS, stride=32), :]
            code = jnp.round((high + low) * scale).astype(i32)
            phase_ref[pl.ds(64 * r, 64), pl.ds(128 * kk, 128)] = code.astype(jnp.int16)


def unpack(got):
    return pl.pallas_call(
        unpack_kernel,
        out_shape=(
            jax.ShapeDtypeStruct((2, 128, 512), bf16),
            jax.ShapeDtypeStruct((128, 512), jnp.int16),
        ),
        scratch_shapes=[pltpu.VMEM((SLOTS * 32, 128), f32)],
        compiler_params=pltpu.CompilerParams(vmem_limit_bytes=16 * MIB),
        name="unpack",
    )(got)


def tables_kernel(fine_ref, coarse_ref, first_ref, second_ref, last_ref):
    for table, (out, blocks) in enumerate(((first_ref, 8), (second_ref, 8), (last_ref, 4))):

        def block(beta, carry, table=table, out=out):
            fc = fine_ref[2 * table]
            fs = fine_ref[2 * table + 1]
            cc = coarse_ref[2 * table, pl.ds(beta, 1), :]
            cs = coarse_ref[2 * table + 1, pl.ds(beta, 1), :]
            rows = pl.ds(pl.multiple_of(64 * beta, 64), 64)
            for kind, value in enumerate((fc * cc - fs * cs, fs * cc + fc * cs)):
                high, low = split(value)
                out[2 * kind, rows, :] = high
                out[2 * kind + 1, rows, :] = low
            return carry

        lax.fori_loop(0, blocks, block, 0)


def tables(fine_table, coarse_table):
    return pl.pallas_call(
        tables_kernel,
        out_shape=(
            jax.ShapeDtypeStruct((4, 512, 512), bf16),
            jax.ShapeDtypeStruct((4, 512, 512), bf16),
            jax.ShapeDtypeStruct((4, 256, 512), bf16),
        ),
        compiler_params=pltpu.CompilerParams(vmem_limit_bytes=16 * MIB),
        cost_estimate=pl.CostEstimate(flops=8000000, bytes_accessed=6 * MIB, transcendentals=0),
        name="tables",
    )(fine_table, coarse_table)


def dot(a, b):
    return jnp.dot(a, b, preferred_element_type=f32)


def dot3(a, b):
    return dot(a[0], b[0]) + dot(a[0], b[1]) + dot(a[1], b[0])


ROWS = 128


def sin_cos(code):
    quadrant = (code + 32768) >> 16
    rest = (code - (quadrant << 16)).astype(f32) * (2.0 * math.pi / NFFT)
    sq = rest * rest
    sine = rest + rest * sq * (
        -1.6666654611e-1 + sq * (8.3321608736e-3 + sq * -1.9515295891e-4)
    )
    cosine = 1.0 + sq * (
        -0.5 + sq * (4.166664568298827e-2 + sq * (-1.388731625493765e-3 + sq * 2.443315711809948e-5))
    )
    odd = (quadrant & 1) == 1
    sin_out = jnp.where(odd, cosine, sine)
    cos_out = jnp.where(odd, sine, cosine)
    sin_out = jnp.where((quadrant & 2) == 2, -sin_out, sin_out)
    cos_out = jnp.where(((quadrant + 1) & 2) == 2, -cos_out, cos_out)
    return sin_out, cos_out


def transform_kernel(
    shift_ref, xa, xb, xc, xd, pa, pb, pc, pd, first, second, last, fine, coarse,
    out_ref, xre, xim, phases, zhi, zlo, fine_own, coarse_own,
):
    core = lax.axis_index("core")
    xl = lax.axis_index("xl")
    slot = (lax.axis_index("z") * 4 + lax.axis_index("y")) * 2 + lax.axis_index("xh")
    series = jnp.where(slot < SERIES, slot, slot - SERIES)
    shift = shift_ref[series // 2]
    for x_in, p_in, dc, dx in ((xa, pa, 0, 0), (xb, pb, 0, 1), (xc, pc, 1, 0), (xd, pd, 1, 1)):
        place = ((core + dc) % 2) * 2 + (xl + dx) % 2
        rows = pl.ds(pl.multiple_of(place * 128, 128), 128)
        xre[rows, :] = x_in[0]
        xim[rows, :] = x_in[1]
        phases[rows, :] = p_in[...]
    quarter = pl.ds(pl.multiple_of((core * 2 + xl) * 128, 128), 128)
    coarse_own[...] = coarse[6:8, :, quarter]
    fine_own[...] = fine[6:8, :, quarter]
    column = lax.broadcasted_iota(i32, (1, 512), 1)
    column_term = ((column * shift) & 511) * 512

    def block(index, carry):
        rows = pl.ds(pl.multiple_of(ROWS * index, ROWS), ROWS)
        wc = (first[0, rows, :], first[1, rows, :])
        ws = (first[2, rows, :], first[3, rows, :])
        re, im = xre[...], xim[...]
        real = dot(wc[0], re) + dot(wc[1], re) + dot(ws[0], im) + dot(ws[1], im)
        imag = dot(wc[0], im) + dot(wc[1], im) - dot(ws[0], re) - dot(ws[1], re)
        tcs, tss, tcq, tsq = [], [], [], []
        for half in range(ROWS // 64):
            beta = index * (ROWS // 64) + half
            cc = coarse[6, pl.ds(beta, 1), :]
            cs = coarse[7, pl.ds(beta, 1), :]
            tcs.append(fine[6] * cc - fine[7] * cs)
            tss.append(fine[7] * cc + fine[6] * cs)
            cc = coarse_own[0, pl.ds(beta, 1), :]
            cs = coarse_own[1, pl.ds(beta, 1), :]
            fc = fine_own[0]
            fs = fine_own[1]
            tcq.append(fc * cc - fs * cs)
            tsq.append(fs * cc + fc * cs)
        tc, ts = jnp.concatenate(tcs, 0), jnp.concatenate(tss, 0)
        yre = split(real * tc + imag * ts)
        yim = split(imag * tc - real * ts)
        w2c = (second[0], second[1])
        w2s = (second[2], second[3])
        real = dot3(yre, w2c) + dot3(yim, w2s)
        imag = dot3(yim, w2c) - dot3(yre, w2s)
        row = lax.broadcasted_iota(i32, (ROWS, 1), 0) + ROWS * index
        m = row & 63
        k1 = 16 * (m >> 1) + 4 * (m & 1) + 8 * (row >> 8) + 2 * ((row >> 7) & 1) + ((row >> 6) & 1)
        code = phases[rows, :].astype(i32) * 4 + k1 * shift + column_term
        sine, cosine = sin_cos(code)
        ure = split(real * cosine - imag * sine)
        uim = split(real * sine + imag * cosine)
        w3c = (second[0, :, quarter], second[1, :, quarter])
        w3s = (second[2, :, quarter], second[3, :, quarter])
        w3 = [jnp.concatenate([c, s], 1) for c, s in zip(w3c, w3s)]
        from_re = dot3(ure, w3)
        from_im = dot3(uim, w3)
        real = from_re[:, :128] - from_im[:, 128:]
        imag = from_re[:, 128:] + from_im[:, :128]
        tc, ts = jnp.concatenate(tcq, 0), jnp.concatenate(tsq, 0)
        high, low = split(real * tc - imag * ts)
        zhi[rows, :128] = high
        zlo[rows, :128] = low
        high, low = split(real * ts + imag * tc)
        zhi[rows, 128:] = high
        zlo[rows, 128:] = low
        return carry

    lax.fori_loop(0, 512 // ROWS, block, 0)
    z = (zhi[...], zlo[...])
    by_cos = dot3((last[0], last[1]), z)
    by_sin = dot3((last[2], last[3]), z)
    real = by_cos[:, :128] - by_sin[:, 128:]
    imag = by_sin[:, :128] + by_cos[:, 128:]
    out_ref[...] = real * real + imag * imag


def transform(shifts, xs, phases, first, second, last, fine_table, coarse_table):
    vmem = pl.BlockSpec(memory_space=pltpu.VMEM)
    return pl.pallas_call(
        transform_kernel,
        out_shape=jax.ShapeDtypeStruct((256, 128), f32),
        in_specs=[pl.BlockSpec(memory_space=pltpu.SMEM)] + [vmem] * 13,
        scratch_shapes=[
            pltpu.VMEM((512, 512), bf16),
            pltpu.VMEM((512, 512), bf16),
            pltpu.VMEM((512, 512), jnp.int16),
            pltpu.VMEM((512, 256), bf16),
            pltpu.VMEM((512, 256), bf16),
            pltpu.VMEM((2, 64, 128), f32),
            pltpu.VMEM((2, 8, 128), f32),
        ],
        compiler_params=pltpu.CompilerParams(vmem_limit_bytes=40 * MIB),
        cost_estimate=pl.CostEstimate(flops=7000000000, bytes_accessed=8 * MIB, transcendentals=0),
        name="transform",
    )(shifts, *xs, *phases, first, second, last, fine_table, coarse_table)


def combine_kernel(group_ref, power_ref, out_ref):
    lane = lax.broadcasted_iota(i32, (16, 256), 1)
    sub = lax.broadcasted_iota(i32, (16, 256), 0)
    slot = (lane // 8) * 2 + (lane // 2) % 2
    quarter = ((lane // 4) % 2) * 2 + lane % 2
    channel = slot // 2
    owner = jnp.zeros((16, 256), i32) - 1
    counts = [jnp.int32(0)] * GROUPS
    for c in range(CHANS):
        g = group_ref[c]
        owner = jnp.where(channel == c, g, owner)
        counts = [n + (g == k).astype(i32) for k, n in enumerate(counts)]
    group = sub % 4
    count = jnp.zeros((16, 256), i32)
    for k in range(GROUPS):
        count = jnp.where(group == k, counts[k], count)
    scale = 1.0 / (2.0 * count.astype(f32)) * (1.0 / NFFT) * (1.0 / NFFT)
    weight = jnp.where((owner == group) & (quarter == sub // 4), scale, 0.0)
    total = jnp.dot(weight, power_ref[...], precision=lax.Precision.HIGHEST, preferred_element_type=f32)
    for j in range(4):
        out_ref[:, pl.ds(128 * j, 128)] = total[4 * j : 4 * j + 4, :]


def combine(group_of, power):
    return pl.pallas_call(
        combine_kernel,
        out_shape=jax.ShapeDtypeStruct((GROUPS, 512), f32),
        in_specs=[pl.BlockSpec(memory_space=pltpu.SMEM), pl.BlockSpec(memory_space=pltpu.VMEM)],
        name="combine",
    )(group_of, power)


def on_device(voltages, chirp_phase, intersection, group_of):
    fine_np, coarse_np = table_factors()
    fine_table, coarse_table = jnp.asarray(fine_np), jnp.asarray(coarse_np)
    got = lax.all_to_all(pack(voltages, chirp_phase), SPREAD, 0, 0, tiled=True)
    own_x, own_p = unpack(got)
    own_x, own_p, fine_late = lax.optimization_barrier((own_x, own_p, fine_table))
    xb = lax.ppermute(own_x, "xl", SWAP)
    pb = lax.ppermute(own_p, "xl", SWAP)
    xc = lax.ppermute(own_x, "core", SWAP)
    pc = lax.ppermute(own_p, "core", SWAP)
    first, second, last = tables(fine_late, coarse_table)
    xd = lax.ppermute(xb, "core", SWAP)
    pd = lax.ppermute(pb, "core", SWAP)
    power = transform(
        intersection, (own_x, xb, xc, xd), (own_p, pb, pc, pd), first, second, last, fine_table, coarse_table
    )
    spread = lax.all_to_all(power.reshape(256, 1, 128), AXES, 0, 0, tiled=True)
    return combine(group_of, spread.reshape(256, 128)).reshape(1, GROUPS, 512)


def solution(mesh):
    inner = Mesh(mesh.devices.reshape(8, 4, 2, 2, 2), AXES)
    in_specs = (P(None, None, None, None, AXES), P(None, ("z", "y", "core"), None), P(), P())
    return jax.shard_map(
        on_device, mesh=inner, in_specs=in_specs, out_specs=P(None, None, AXES), check_vma=False
    )
```

```python
import functools
import math

import jax
import jax.numpy as jnp
import numpy as np
from jax import lax
from jax.experimental import pallas as pl
from jax.experimental.pallas import tpu as pltpu
from jax.sharding import Mesh
from jax.sharding import PartitionSpec as P

NFFT = 262144
F1 = 512
F2 = 512
CHANS = 24
POLS = 2
SERIES = CHANS * POLS
SLOTS = 64
GROUPS = 4
AXES = ("z", "y", "core", "xh", "xl")
SPREAD = ("z", "y", "xh")
SWAP = [(0, 1), (1, 0)]
MIB = 1 << 20
ROWS = 128

f32 = jnp.float32
bf16 = jnp.bfloat16
i32 = jnp.int32


def cos_sin(index, period):
    angle = 2.0 * np.pi * (index % period) / period
    return np.stack([np.cos(angle), np.sin(angle)]).astype(np.float32)


@functools.cache
def table_factors():
    beta = np.arange(8)
    m = np.arange(64)
    fine = 16 * (m // 2) + 4 * (m % 2)
    coarse = 8 * (beta // 4) + 2 * (beta // 2 % 2) + beta % 2
    place = coarse.reshape(4, 2)
    sample_row = np.concatenate([(place[:, jj, None] + fine[None, :]).reshape(-1) for jj in range(2)])
    low = fine[:32]
    high_part = np.concatenate([coarse, 256 + coarse])
    k1 = (high_part[:, None] + low[None, :]).reshape(-1)
    half = np.arange(256)
    sample_column = np.concatenate([2 * half, 2 * half + 1])
    quarter = np.arange(128)
    out_column = 4 * quarter[None, :] + np.arange(4)[:, None]

    def outer(rows, columns, period):
        return cos_sin(rows[:, None] * columns[None, :], period)

    def outers(rows, columns, period):
        return np.stack([outer(rows, c, period) for c in columns])

    even_odd = np.concatenate([128 * np.arange(4), 128 * np.arange(4) + 1])
    return dict(
        w1=(outer(low, sample_row, F1), outer(coarse, sample_row, F1)),
        w2=(outer(2 * m, half, F2), outer(even_odd, half, F2)),
        w4=(outer(m, k1, F1), outer(64 * np.arange(4), k1, F1)),
        m3=outers(quarter, out_column, F2),
        t1=(outer(low, sample_column, NFFT), outer(high_part, sample_column, NFFT)),
        t3=(outers(low, out_column, NFFT), outers(high_part, out_column, NFFT)),
    )


def split(value):
    high = value.astype(bf16)
    return high, (value - high.astype(f32)).astype(bf16)


def turned(fine, coarse):
    return fine[0] * coarse[0] - fine[1] * coarse[1], fine[1] * coarse[0] + fine[0] * coarse[1]


def pack_kernel(v_hbm, c_hbm, out_ref, v_ref, c_ref, wide, narrow, tall, v_sem, c_sem):
    v_copy = pltpu.make_async_copy(v_hbm, v_ref, v_sem)
    c_copy = pltpu.make_async_copy(c_hbm, c_ref, c_sem)
    v_copy.start()
    c_copy.start()
    x_pos = 2 * lax.axis_index("xh") + lax.axis_index("xl")
    into = lax.broadcasted_iota(i32, (256, 256), 1)
    sample = lax.broadcasted_iota(i32, (256, 256), 0)
    pick = (sample == 2 * (into & 127) + (into >> 7)).astype(f32).astype(bf16)
    v_copy.wait()
    samples = v_ref[...].reshape(SERIES * 2, 1024)
    for jj in range(2):
        for u in range(2):
            start = 512 * jj + 256 * u
            piece = jnp.dot(samples[:, start : start + 256], pick, preferred_element_type=f32)
            for odd in range(2):
                i = 4 * jj + 2 * odd + u
                wide[pl.ds(SERIES * 2 * i, SERIES * 2), :] = piece[:, 128 * odd : 128 * odd + 128]
    for reim in range(2):
        for i in range(8):
            rows = wide[pl.ds(SERIES * 2 * i + reim, SERIES, stride=2), :]
            tall[pl.ds(reim * 8 + i, SERIES, stride=32), :] = rows
    c_copy.wait()
    for kk in range(4):
        narrow[pl.ds(CHANS * 8 * kk, CHANS * 8), :] = c_ref[:, pl.ds(128 * kk, 128)]
    for r in range(2):
        for kk in range(4):
            phase = narrow[pl.ds(CHANS * 8 * kk + 2 * x_pos + r, CHANS, stride=8), :]
            high = phase.astype(bf16).astype(f32)
            low = phase - high
            for pol in range(2):
                base = pol * 32 + 16 + r * 4 + kk
                tall[pl.ds(base, CHANS, stride=64), :] = high
                tall[pl.ds(base + 8, CHANS, stride=64), :] = low
    packed = tall[...].astype(bf16).reshape(SERIES, 32, 128)
    out_ref[pl.ds(0, SERIES)] = packed
    out_ref[pl.ds(SERIES, SLOTS - SERIES)] = packed[: SLOTS - SERIES]


def pack(voltages, chirp):
    return pl.pallas_call(
        pack_kernel,
        out_shape=jax.ShapeDtypeStruct((SLOTS, 32, 128), bf16),
        in_specs=[pl.BlockSpec(memory_space=pltpu.HBM)] * 2,
        scratch_shapes=[
            pltpu.VMEM((CHANS, POLS, 2, 1024), bf16),
            pltpu.VMEM((CHANS * 8, 512), f32),
            pltpu.VMEM((SERIES * 16, 128), f32),
            pltpu.VMEM((CHANS * 32, 128), f32),
            pltpu.VMEM((SERIES * 32, 128), f32),
            pltpu.SemaphoreType.DMA,
            pltpu.SemaphoreType.DMA,
        ],
        compiler_params=pltpu.CompilerParams(vmem_limit_bytes=16 * MIB),
        name="pack",
    )(voltages.reshape(CHANS, POLS, 2, 1024), chirp.reshape(CHANS * 8, 512))


def unpack_kernel(got_ref, x_ref, phase_ref, tall):
    tall[...] = got_ref[...].reshape(SLOTS * 32, 128).astype(f32)
    for reim in range(2):
        for i in range(8):
            rows = tall[pl.ds(reim * 8 + i, SLOTS, stride=32), :]
            x_ref[reim, pl.ds(64 * (i // 4), 64), pl.ds(128 * (i % 4), 128)] = rows.astype(bf16)
    scale = 65536.0 / (2.0 * math.pi)
    for r in range(2):
        for kk in range(4):
            high = tall[pl.ds(16 + r * 4 + kk, SLOTS, stride=32), :]
            low = tall[pl.ds(24 + r * 4 + kk, SLOTS, stride=32), :]
            code = jnp.round((high + low) * scale).astype(i32)
            phase_ref[pl.ds(64 * r, 64), pl.ds(128 * kk, 128)] = code.astype(jnp.int16)


def unpack(got):
    return pl.pallas_call(
        unpack_kernel,
        out_shape=(
            jax.ShapeDtypeStruct((2, 128, 512), bf16),
            jax.ShapeDtypeStruct((128, 512), jnp.int16),
        ),
        scratch_shapes=[pltpu.VMEM((SLOTS * 32, 128), f32)],
        compiler_params=pltpu.CompilerParams(vmem_limit_bytes=16 * MIB),
        name="unpack",
    )(got)


def tables_kernel(group_ref, f1, c1, f2, c2, f4, c4, m3, w1_ref, w2_ref, w4_ref, m3_ref, weight_ref, order_ref):
    for fine, coarse, out, height, blocks in (
        (f1, c1, w1_ref, 32, 8),
        (f2, c2, w2_ref, 64, 8),
        (f4, c4, w4_ref, 64, 4),
    ):

        def block(beta, carry, fine=fine, coarse=coarse, out=out, height=height):
            row = pl.ds(beta, 1)
            rows = pl.ds(pl.multiple_of(height * beta, height), height)
            values = turned((fine[0], fine[1]), (coarse[0, row, :], coarse[1, row, :]))
            for kind, value in enumerate(values):
                high, low = split(value)
                out[2 * kind, rows, :] = high
                out[2 * kind + 1, rows, :] = low
            return carry

        lax.fori_loop(0, blocks, block, 0)
    j = 2 * lax.axis_index("core") + lax.axis_index("xl")
    cosine, sine = m3[j, 0], m3[j, 1]
    for row, column, value in ((0, 0, cosine), (0, 1, sine), (1, 0, -sine), (1, 1, cosine)):
        high, low = split(value)
        m3_ref[0, pl.ds(128 * row, 128), pl.ds(128 * column, 128)] = high
        m3_ref[1, pl.ds(128 * row, 128), pl.ds(128 * column, 128)] = low
    source = lax.broadcasted_iota(i32, (256, 128), 0)
    channel = (source // 8 * 2 + source // 2 % 2) // 2
    owner = jnp.zeros((256, 128), i32) - 1
    counts = [jnp.int32(0)] * GROUPS
    for c in range(CHANS):
        g = group_ref[c]
        owner = jnp.where(channel == c, g, owner)
        counts = [n + (g == k).astype(i32) for k, n in enumerate(counts)]
    for k in range(GROUPS):
        count = jnp.broadcast_to(counts[k], (256, 128)).astype(f32)
        scale = 1.0 / (2.0 * count) * (1.0 / NFFT) * (1.0 / NFFT)
        weight_ref[k] = jnp.where(owner == k, scale, 0.0)
    source = lax.broadcasted_iota(i32, (512, 512), 0)
    column = lax.broadcasted_iota(i32, (512, 512), 1)
    order_ref[...] = (column == 4 * (source & 127) + (source >> 7)).astype(f32).astype(bf16)


def tables(group_of, factors):
    vmem = pl.BlockSpec(memory_space=pltpu.VMEM)
    flat = [factors["w1"][0], factors["w1"][1], factors["w2"][0], factors["w2"][1]]
    flat += [factors["w4"][0], factors["w4"][1], factors["m3"]]
    return pl.pallas_call(
        tables_kernel,
        out_shape=(
            jax.ShapeDtypeStruct((4, 256, 512), bf16),
            jax.ShapeDtypeStruct((4, 512, 256), bf16),
            jax.ShapeDtypeStruct((4, 256, 512), bf16),
            jax.ShapeDtypeStruct((2, 256, 256), bf16),
            jax.ShapeDtypeStruct((GROUPS, 256, 128), f32),
            jax.ShapeDtypeStruct((512, 512), bf16),
        ),
        in_specs=[pl.BlockSpec(memory_space=pltpu.SMEM)] + [vmem] * 7,
        compiler_params=pltpu.CompilerParams(vmem_limit_bytes=16 * MIB),
        cost_estimate=pl.CostEstimate(flops=8000000, bytes_accessed=6 * MIB, transcendentals=0),
        name="tables",
    )(group_of, *flat)


def dot(a, b):
    return jnp.dot(a, b, preferred_element_type=f32)


def dot3(a, b):
    return dot(a[0], b[0]) + dot(a[0], b[1]) + dot(a[1], b[0])


def sin_cos(code):
    quadrant = (code + 32768) >> 16
    rest = (code - (quadrant << 16)).astype(f32) * (2.0 * math.pi / NFFT)
    sq = rest * rest
    sine = rest + rest * sq * (
        -1.6666654611e-1 + sq * (8.3321608736e-3 + sq * -1.9515295891e-4)
    )
    cosine = 1.0 + sq * (
        -0.5 + sq * (4.166664568298827e-2 + sq * (-1.388731625493765e-3 + sq * 2.443315711809948e-5))
    )
    odd = (quadrant & 1) == 1
    sin_out = jnp.where(odd, cosine, sine)
    cos_out = jnp.where(odd, sine, cosine)
    sin_out = jnp.where((quadrant & 2) == 2, -sin_out, sin_out)
    cos_out = jnp.where(((quadrant + 1) & 2) == 2, -cos_out, cos_out)
    return sin_out, cos_out


def partner(dc, dx):
    core = (lax.axis_index("core") + dc) % 2
    xl = (lax.axis_index("xl") + dx) % 2
    return core * 2 + xl


def forward_kernel(xa, xb, xc, xd, w1, w2, fine, coarse, out_ref, xre, xim):
    for x_in, dc, dx in ((xa, 0, 0), (xb, 0, 1), (xc, 1, 0), (xd, 1, 1)):
        place = partner(dc, dx)
        for jj in range(2):
            rows = pl.ds(pl.multiple_of(jj * 256 + place * 64, 64), 64)
            xre[rows, :] = x_in[0, pl.ds(64 * jj, 64), :]
            xim[rows, :] = x_in[1, pl.ds(64 * jj, 64), :]
    for block in range(2):
        parts = []
        for jj in range(2):
            rows, columns = pl.ds(128 * block, 128), pl.ds(256 * jj, 256)
            c0, c1, s0, s1 = (w1[k, rows, columns] for k in range(4))
            re, im = xre[columns, :], xim[columns, :]
            real = dot(c0, re) + dot(c1, re) + dot(s0, im) + dot(s1, im)
            imag = dot(c0, im) + dot(c1, im) - (dot(s0, re) + dot(s1, re))
            parts.append((real, imag))
        (even_re, even_im), (odd_re, odd_im) = parts
        real = jnp.concatenate([even_re + odd_re, even_re - odd_re], 0)
        imag = jnp.concatenate([even_im + odd_im, even_im - odd_im], 0)
        tcs, tss = [], []
        for u in range(2):
            for beta in range(4):
                row = pl.ds(8 * u + 4 * block + beta, 1)
                tc, ts = turned((fine[0], fine[1]), (coarse[0, row, :], coarse[1, row, :]))
                tcs.append(tc)
                tss.append(ts)
        tc, ts = jnp.concatenate(tcs, 0), jnp.concatenate(tss, 0)
        yre = split(real * tc + imag * ts)
        yim = split(imag * tc - real * ts)
        parts = []
        for odd in range(2):
            columns = slice(256 * odd, 256 * odd + 256)
            re = (yre[0][:, columns], yre[1][:, columns])
            im = (yim[0][:, columns], yim[1][:, columns])
            rows = pl.ds(256 * odd, 256)
            c = (w2[0, rows, :], w2[1, rows, :])
            s = (w2[2, rows, :], w2[3, rows, :])
            parts.append((dot3(re, c) + dot3(im, s), dot3(im, c) - dot3(re, s)))
        for k in range(2):
            even, odd = parts[0][k], parts[1][k]
            for u in range(2):
                rows = pl.ds(256 * u + 128 * block, 128)
                half = slice(128 * u, 128 * u + 128)
                out_ref[k, rows, pl.ds(0, 256)] = even[half] + odd[half]
                out_ref[k, rows, pl.ds(256, 256)] = even[half] - odd[half]


def forward(xs, w1, w2, factors):
    return pl.pallas_call(
        forward_kernel,
        out_shape=jax.ShapeDtypeStruct((2, 512, 512), f32),
        scratch_shapes=[pltpu.VMEM((512, 512), bf16), pltpu.VMEM((512, 512), bf16)],
        compiler_params=pltpu.CompilerParams(vmem_limit_bytes=24 * MIB),
        cost_estimate=pl.CostEstimate(flops=2700000000, bytes_accessed=5 * MIB, transcendentals=0),
        name="forward",
    )(*xs, w1, w2, factors["t1"][0], factors["t1"][1])


def inverse_kernel(shift_ref, spec, pa, pb, pc, pd, m3, w4, fine, coarse, out_ref, phases, zhi, zlo):
    slot = (lax.axis_index("z") * 4 + lax.axis_index("y")) * 2 + lax.axis_index("xh")
    series = jnp.where(slot < SERIES, slot, slot - SERIES)
    shift = shift_ref[series // 2]
    for p_in, dc, dx in ((pa, 0, 0), (pb, 0, 1), (pc, 1, 0), (pd, 1, 1)):
        place = partner(dc, dx)
        for u in range(2):
            for r in range(2):
                rows = pl.ds(pl.multiple_of(256 * u + 64 * place + 32 * r, 32), 32)
                phases[rows, :] = p_in[pl.ds(64 * r + 32 * u, 32), :]
    j = partner(0, 0)
    sign = jnp.where(j % 2 == 0, 1.0, -1.0)
    turn_re = jnp.where(j == 0, 1.0, jnp.where(j == 2, -1.0, 0.0))
    turn_im = jnp.where(j == 1, 1.0, jnp.where(j == 3, -1.0, 0.0))
    column = lax.broadcasted_iota(i32, (1, 512), 1)
    column_term = ((column * shift) & 511) * 512
    for block in range(512 // ROWS):
        rows = pl.ds(ROWS * block, ROWS)
        row = lax.broadcasted_iota(i32, (ROWS, 1), 0) + ROWS * block
        beta = row >> 5
        k1 = 256 * (row >> 8) + 8 * ((beta >> 2) & 1) + 2 * ((beta >> 1) & 1) + (beta & 1)
        k1 = k1 + 16 * ((row & 31) >> 1) + 4 * (row & 1)
        code = phases[rows, :].astype(i32) * 4 + k1 * shift + column_term
        sine, cosine = sin_cos(code)
        real, imag = spec[0, rows, :], spec[1, rows, :]
        ure = real * cosine - imag * sine
        uim = real * sine + imag * cosine
        are = ure[:, :128] + sign * ure[:, 256:384]
        aim = uim[:, :128] + sign * uim[:, 256:384]
        bre = ure[:, 128:256] + sign * ure[:, 384:]
        bim = uim[:, 128:256] + sign * uim[:, 384:]
        folded = jnp.concatenate(
            [are + turn_re * bre - turn_im * bim, aim + turn_re * bim + turn_im * bre], 1
        )
        mixed = dot3(split(folded), (m3[0], m3[1]))
        real, imag = mixed[:, :128], mixed[:, 128:]
        tcs, tss = [], []
        for b in range(ROWS // 32):
            at = pl.ds(block * (ROWS // 32) + b, 1)
            tc, ts = turned((fine[j, 0], fine[j, 1]), (coarse[j, 0, at, :], coarse[j, 1, at, :]))
            tcs.append(tc)
            tss.append(ts)
        tc, ts = jnp.concatenate(tcs, 0), jnp.concatenate(tss, 0)
        high, low = split(real * tc - imag * ts)
        zhi[rows, :128] = high
        zlo[rows, :128] = low
        high, low = split(real * ts + imag * tc)
        zhi[rows, 128:] = high
        zlo[rows, 128:] = low
    z = (zhi[...], zlo[...])
    by_cos = dot3((w4[0], w4[1]), z)
    by_sin = dot3((w4[2], w4[3]), z)
    real = by_cos[:, :128] - by_sin[:, 128:]
    imag = by_sin[:, :128] + by_cos[:, 128:]
    out_ref[...] = real * real + imag * imag


def inverse(shifts, spec, phases, m3, w4, factors):
    vmem = pl.BlockSpec(memory_space=pltpu.VMEM)
    return pl.pallas_call(
        inverse_kernel,
        out_shape=jax.ShapeDtypeStruct((256, 128), f32),
        in_specs=[pl.BlockSpec(memory_space=pltpu.SMEM)] + [vmem] * 9,
        scratch_shapes=[
            pltpu.VMEM((512, 512), jnp.int16),
            pltpu.VMEM((512, 256), bf16),
            pltpu.VMEM((512, 256), bf16),
        ],
        compiler_params=pltpu.CompilerParams(vmem_limit_bytes=24 * MIB),
        cost_estimate=pl.CostEstimate(flops=800000000, bytes_accessed=4 * MIB, transcendentals=0),
        name="inverse",
    )(shifts, spec, *phases, m3, w4, factors["t3"][0], factors["t3"][1])


def combine_kernel(power_ref, weight_ref, order_ref, out_ref):
    rows = []
    for g in range(GROUPS):
        total = jnp.sum((weight_ref[g] * power_ref[...]).reshape(32, 8, 128), axis=0)
        places = [total[4 * c + x : 4 * c + x + 1] + total[4 * c + x + 2 : 4 * c + x + 3] for c in range(2) for x in range(2)]
        rows.append(jnp.concatenate(places, 1))
    total = jnp.concatenate(rows, 0)
    high = total.astype(bf16).astype(f32)
    rest = total - high
    middle = rest.astype(bf16).astype(f32)
    pieces = jnp.concatenate([high, middle, rest - middle, jnp.zeros_like(high)], 0).astype(bf16)
    ordered = dot(pieces, order_ref[...])
    out_ref[...] = ordered[0:4] + ordered[4:8] + ordered[8:12]


def combine(power, weight, order):
    return pl.pallas_call(
        combine_kernel,
        out_shape=jax.ShapeDtypeStruct((GROUPS, 512), f32),
        compiler_params=pltpu.CompilerParams(vmem_limit_bytes=8 * MIB),
        name="combine",
    )(power, weight, order)


def on_device(voltages, chirp_phase, intersection, group_of):
    factors = jax.tree.map(jnp.asarray, table_factors())
    w1, w2, w4, m3, weight, order = tables(group_of, factors)
    got = lax.all_to_all(pack(voltages, chirp_phase), SPREAD, 0, 0, tiled=True)
    own_x, own_p = unpack(got)
    xb = lax.ppermute(own_x, "xl", SWAP)
    xc = lax.ppermute(own_x, "core", SWAP)
    xd = lax.ppermute(xb, "core", SWAP)
    late_p, _ = lax.optimization_barrier((own_p, xb))
    pb = lax.ppermute(late_p, "xl", SWAP)
    pc = lax.ppermute(late_p, "core", SWAP)
    pd = lax.ppermute(late_p, ("core", "xl"), [(i, 3 - i) for i in range(4)])
    spec = forward((own_x, xb, xc, xd), w1, w2, factors)
    power = inverse(intersection, spec, (own_p, pb, pc, pd), m3, w4, factors)
    spread = lax.all_to_all(power.reshape(256, 1, 128), AXES, 0, 0, tiled=True)
    return combine(spread.reshape(256, 128), weight, order).reshape(1, GROUPS, 512)


def solution(mesh):
    inner = Mesh(mesh.devices.reshape(8, 4, 2, 2, 2), AXES)
    in_specs = (P(None, None, None, None, AXES), P(None, ("z", "y", "core"), None), P(), P())
    return jax.shard_map(
        on_device, mesh=inner, in_specs=in_specs, out_specs=P(None, None, AXES), check_vma=False
    )
```

```python
import functools
import math

import jax
import jax.numpy as jnp
import numpy as np
from jax import lax
from jax.experimental import pallas as pl
from jax.experimental.pallas import tpu as pltpu
from jax.sharding import Mesh
from jax.sharding import PartitionSpec as P

NFFT = 262144
F1 = 512
F2 = 512
CHANS = 24
POLS = 2
SERIES = CHANS * POLS
SLOTS = 64
GROUPS = 4
AXES = ("z", "y", "core", "xh", "xl")
SPREAD = ("z", "y", "xh")
SWAP = [(0, 1), (1, 0)]
MIB = 1 << 20
ROWS = 128
CHUNK = 24

f32 = jnp.float32
bf16 = jnp.bfloat16
i32 = jnp.int32


def cos_sin(index, period):
    angle = 2.0 * np.pi * (index % period) / period
    return np.stack([np.cos(angle), np.sin(angle)]).astype(np.float32)


@functools.cache
def table_factors():
    beta = np.arange(8)
    m = np.arange(64)
    fine = 16 * (m // 2) + 4 * (m % 2)
    coarse = 8 * (beta // 4) + 2 * (beta // 2 % 2) + beta % 2
    place = coarse.reshape(4, 2)
    sample_row = np.concatenate([(place[:, jj, None] + fine[None, :]).reshape(-1) for jj in range(2)])
    low = fine[:32]
    high_part = np.concatenate([coarse, 256 + coarse])
    k1 = (high_part[:, None] + low[None, :]).reshape(-1)
    half = np.arange(256)
    sample_column = np.concatenate([2 * half, 2 * half + 1])
    quarter = np.arange(128)
    out_column = 4 * quarter[None, :] + np.arange(4)[:, None]

    def outer(rows, columns, period):
        return cos_sin(rows[:, None] * columns[None, :], period)

    def outers(rows, columns, period):
        return np.stack([outer(rows, c, period) for c in columns])

    even_odd = np.concatenate([128 * np.arange(4), 128 * np.arange(4) + 1])
    return dict(
        w1=(outer(low, sample_row, F1), outer(coarse, sample_row, F1)),
        w2=(outer(2 * m, half, F2), outer(even_odd, half, F2)),
        w4=(outer(m, k1, F1), outer(64 * np.arange(4), k1, F1)),
        m3=outers(quarter, out_column, F2),
        t1=(outer(low, sample_column, NFFT), outer(high_part, sample_column, NFFT)),
        t3=(outers(low, out_column, NFFT), outers(high_part, out_column, NFFT)),
    )


def split(value):
    high = value.astype(bf16)
    return high, (value - high.astype(f32)).astype(bf16)


def turned(fine, coarse):
    return fine[0] * coarse[0] - fine[1] * coarse[1], fine[1] * coarse[0] + fine[0] * coarse[1]


def encode(phase):
    steps = jnp.round(phase * (16384.0 / math.pi))
    size = jnp.abs(steps).astype(i32)
    value = (1.0 + (size & 127).astype(f32) * (1.0 / 128.0)) * 2.0**-64
    for k in range(7):
        value = jnp.where(((size >> (7 + k)) & 1) == 1, value * 2.0 ** (1 << k), value)
    return jnp.where(steps < 0.0, -value, value)


def decode(coded):
    value = jnp.abs(coded) * 2.0**64
    size = jnp.zeros_like(value)
    for k in reversed(range(7)):
        large = value >= 2.0 ** (1 << k)
        value = jnp.where(large, value * 2.0 ** -(1 << k), value)
        size = jnp.where(large, size + 256.0 * (1 << k), size)
    size = size + (value - 1.0) * 256.0
    return jnp.where(coded < 0.0, -size, size).astype(i32)


def pack_kernel(v_hbm, c_hbm, out_ref, v_ref, c_ref, wide, narrow, tall, v_sem, c_sem):
    v_copy = pltpu.make_async_copy(v_hbm, v_ref, v_sem)
    c_copy = pltpu.make_async_copy(c_hbm, c_ref, c_sem)
    v_copy.start()
    c_copy.start()
    x_pos = 2 * lax.axis_index("xh") + lax.axis_index("xl")
    into = lax.broadcasted_iota(i32, (256, 256), 1)
    sample = lax.broadcasted_iota(i32, (256, 256), 0)
    pick = (sample == 2 * (into & 127) + (into >> 7)).astype(f32).astype(bf16)
    v_copy.wait()
    samples = v_ref[...].reshape(SERIES * 2, 1024)
    for jj in range(2):
        for u in range(2):
            start = 512 * jj + 256 * u
            piece = jnp.dot(samples[:, start : start + 256], pick, preferred_element_type=f32)
            for odd in range(2):
                i = 4 * jj + 2 * odd + u
                wide[pl.ds(SERIES * 2 * i, SERIES * 2), :] = piece[:, 128 * odd : 128 * odd + 128]
    for reim in range(2):
        for i in range(8):
            rows = wide[pl.ds(SERIES * 2 * i + reim, SERIES, stride=2), :]
            tall[pl.ds(reim * 8 + i, SERIES, stride=CHUNK), :] = rows
    c_copy.wait()
    for kk in range(4):
        narrow[pl.ds(CHANS * 8 * kk, CHANS * 8), :] = c_ref[:, pl.ds(128 * kk, 128)]
    for r in range(2):
        for kk in range(4):
            phase = narrow[pl.ds(CHANS * 8 * kk + 2 * x_pos + r, CHANS, stride=8), :]
            coded = encode(phase)
            for pol in range(2):
                base = pol * CHUNK + 16 + r * 4 + kk
                tall[pl.ds(base, CHANS, stride=2 * CHUNK), :] = coded
    packed = tall[...].astype(bf16).reshape(SERIES, CHUNK, 128)
    out_ref[pl.ds(0, SERIES)] = packed
    out_ref[pl.ds(SERIES, SLOTS - SERIES)] = packed[: SLOTS - SERIES]


def pack(voltages, chirp):
    return pl.pallas_call(
        pack_kernel,
        out_shape=jax.ShapeDtypeStruct((SLOTS, CHUNK, 128), bf16),
        in_specs=[pl.BlockSpec(memory_space=pltpu.HBM)] * 2,
        scratch_shapes=[
            pltpu.VMEM((CHANS, POLS, 2, 1024), bf16),
            pltpu.VMEM((CHANS * 8, 512), f32),
            pltpu.VMEM((SERIES * 16, 128), f32),
            pltpu.VMEM((CHANS * 32, 128), f32),
            pltpu.VMEM((SERIES * CHUNK, 128), f32),
            pltpu.SemaphoreType.DMA,
            pltpu.SemaphoreType.DMA,
        ],
        compiler_params=pltpu.CompilerParams(vmem_limit_bytes=16 * MIB),
        name="pack",
    )(voltages.reshape(CHANS, POLS, 2, 1024), chirp.reshape(CHANS * 8, 512))


def samples_kernel(got_ref, x_ref, tall):
    tall[...] = got_ref[:, pl.ds(0, 16), :].astype(f32).reshape(SLOTS * 16, 128)
    for reim in range(2):
        for i in range(8):
            rows = tall[pl.ds(reim * 8 + i, SLOTS, stride=16), :]
            x_ref[reim, pl.ds(64 * (i // 4), 64), pl.ds(128 * (i % 4), 128)] = rows.astype(bf16)


def samples(got):
    return pl.pallas_call(
        samples_kernel,
        out_shape=jax.ShapeDtypeStruct((2, 128, 512), bf16),
        scratch_shapes=[pltpu.VMEM((SLOTS * 16, 128), f32)],
        compiler_params=pltpu.CompilerParams(vmem_limit_bytes=16 * MIB),
        name="samples",
    )(got)


def phases_kernel(got_ref, phase_ref, tall):
    tall[...] = got_ref[:, pl.ds(16, 8), :].astype(f32).reshape(SLOTS * 8, 128)
    for r in range(2):
        for kk in range(4):
            coded = tall[pl.ds(r * 4 + kk, SLOTS, stride=8), :]
            phase_ref[pl.ds(64 * r, 64), pl.ds(128 * kk, 128)] = decode(coded).astype(jnp.int16)


def phases(got):
    return pl.pallas_call(
        phases_kernel,
        out_shape=jax.ShapeDtypeStruct((128, 512), jnp.int16),
        scratch_shapes=[pltpu.VMEM((SLOTS * 8, 128), f32)],
        compiler_params=pltpu.CompilerParams(vmem_limit_bytes=16 * MIB),
        cost_estimate=pl.CostEstimate(flops=3000000, bytes_accessed=MIB, transcendentals=0),
        name="phases",
    )(got)


def tables_kernel(group_ref, f1, c1, f2, c2, f4, c4, m3, w1_ref, w2_ref, w4_ref, m3_ref, weight_ref, order_ref):
    for fine, coarse, out, height, blocks in (
        (f1, c1, w1_ref, 32, 8),
        (f2, c2, w2_ref, 64, 8),
        (f4, c4, w4_ref, 64, 4),
    ):

        def block(beta, carry, fine=fine, coarse=coarse, out=out, height=height):
            row = pl.ds(beta, 1)
            rows = pl.ds(pl.multiple_of(height * beta, height), height)
            values = turned((fine[0], fine[1]), (coarse[0, row, :], coarse[1, row, :]))
            for kind, value in enumerate(values):
                high, low = split(value)
                out[2 * kind, rows, :] = high
                out[2 * kind + 1, rows, :] = low
            return carry

        lax.fori_loop(0, blocks, block, 0)
    j = 2 * lax.axis_index("core") + lax.axis_index("xl")
    cosine, sine = m3[j, 0], m3[j, 1]
    for row, column, value in ((0, 0, cosine), (0, 1, sine), (1, 0, -sine), (1, 1, cosine)):
        high, low = split(value)
        m3_ref[0, pl.ds(128 * row, 128), pl.ds(128 * column, 128)] = high
        m3_ref[1, pl.ds(128 * row, 128), pl.ds(128 * column, 128)] = low
    source = lax.broadcasted_iota(i32, (256, 128), 0)
    channel = (source // 8 * 2 + source // 2 % 2) // 2
    owner = jnp.zeros((256, 128), i32) - 1
    counts = [jnp.int32(0)] * GROUPS
    for c in range(CHANS):
        g = group_ref[c]
        owner = jnp.where(channel == c, g, owner)
        counts = [n + (g == k).astype(i32) for k, n in enumerate(counts)]
    for k in range(GROUPS):
        count = jnp.broadcast_to(counts[k], (256, 128)).astype(f32)
        scale = 1.0 / (2.0 * count) * (1.0 / NFFT) * (1.0 / NFFT)
        weight_ref[k] = jnp.where(owner == k, scale, 0.0)
    source = lax.broadcasted_iota(i32, (512, 512), 0)
    column = lax.broadcasted_iota(i32, (512, 512), 1)
    order_ref[...] = (column == 4 * (source & 127) + (source >> 7)).astype(f32).astype(bf16)


def tables(group_of, factors):
    vmem = pl.BlockSpec(memory_space=pltpu.VMEM)
    flat = [factors["w1"][0], factors["w1"][1], factors["w2"][0], factors["w2"][1]]
    flat += [factors["w4"][0], factors["w4"][1], factors["m3"]]
    return pl.pallas_call(
        tables_kernel,
        out_shape=(
            jax.ShapeDtypeStruct((4, 256, 512), bf16),
            jax.ShapeDtypeStruct((4, 512, 256), bf16),
            jax.ShapeDtypeStruct((4, 256, 512), bf16),
            jax.ShapeDtypeStruct((2, 256, 256), bf16),
            jax.ShapeDtypeStruct((GROUPS, 256, 128), f32),
            jax.ShapeDtypeStruct((512, 512), bf16),
        ),
        in_specs=[pl.BlockSpec(memory_space=pltpu.SMEM)] + [vmem] * 7,
        compiler_params=pltpu.CompilerParams(vmem_limit_bytes=16 * MIB),
        cost_estimate=pl.CostEstimate(flops=8000000, bytes_accessed=6 * MIB, transcendentals=0),
        name="tables",
    )(group_of, *flat)


def dot(a, b):
    return jnp.dot(a, b, preferred_element_type=f32)


def dot3(a, b):
    return dot(a[0], b[0]) + dot(a[0], b[1]) + dot(a[1], b[0])


def sin_cos(code):
    quadrant = (code + 32768) >> 16
    rest = (code - (quadrant << 16)).astype(f32) * (2.0 * math.pi / NFFT)
    sq = rest * rest
    sine = rest + rest * sq * (
        -1.6666654611e-1 + sq * (8.3321608736e-3 + sq * -1.9515295891e-4)
    )
    cosine = 1.0 + sq * (
        -0.5 + sq * (4.166664568298827e-2 + sq * (-1.388731625493765e-3 + sq * 2.443315711809948e-5))
    )
    odd = (quadrant & 1) == 1
    sin_out = jnp.where(odd, cosine, sine)
    cos_out = jnp.where(odd, sine, cosine)
    sin_out = jnp.where((quadrant & 2) == 2, -sin_out, sin_out)
    cos_out = jnp.where(((quadrant + 1) & 2) == 2, -cos_out, cos_out)
    return sin_out, cos_out


def partner(dc, dx):
    core = (lax.axis_index("core") + dc) % 2
    xl = (lax.axis_index("xl") + dx) % 2
    return core * 2 + xl


def first_kernel(xa, xb, xc, xd, w1, fine, coarse, y_ref, xre, xim):
    for x_in, dc, dx in ((xa, 0, 0), (xb, 0, 1), (xc, 1, 0), (xd, 1, 1)):
        place = partner(dc, dx)
        for jj in range(2):
            rows = pl.ds(pl.multiple_of(jj * 256 + place * 64, 64), 64)
            xre[rows, :] = x_in[0, pl.ds(64 * jj, 64), :]
            xim[rows, :] = x_in[1, pl.ds(64 * jj, 64), :]
    for block in range(2):
        parts = []
        for jj in range(2):
            rows, columns = pl.ds(128 * block, 128), pl.ds(256 * jj, 256)
            c0, c1, s0, s1 = (w1[k, rows, columns] for k in range(4))
            re, im = xre[columns, :], xim[columns, :]
            real = dot(c0, re) + dot(c1, re) + dot(s0, im) + dot(s1, im)
            imag = dot(c0, im) + dot(c1, im) - (dot(s0, re) + dot(s1, re))
            parts.append((real, imag))
        (even_re, even_im), (odd_re, odd_im) = parts
        for u, (real, imag) in enumerate(
            ((even_re + odd_re, even_im + odd_im), (even_re - odd_re, even_im - odd_im))
        ):
            tcs, tss = [], []
            for beta in range(4):
                row = pl.ds(8 * u + 4 * block + beta, 1)
                tc, ts = turned((fine[0], fine[1]), (coarse[0, row, :], coarse[1, row, :]))
                tcs.append(tc)
                tss.append(ts)
            tc, ts = jnp.concatenate(tcs, 0), jnp.concatenate(tss, 0)
            rows = pl.ds(256 * u + 128 * block, 128)
            y_ref[0, rows, :], y_ref[1, rows, :] = split(real * tc + imag * ts)
            y_ref[2, rows, :], y_ref[3, rows, :] = split(imag * tc - real * ts)


def first(xs, w1, factors):
    return pl.pallas_call(
        first_kernel,
        out_shape=jax.ShapeDtypeStruct((4, 512, 512), bf16),
        scratch_shapes=[pltpu.VMEM((512, 512), bf16), pltpu.VMEM((512, 512), bf16)],
        compiler_params=pltpu.CompilerParams(vmem_limit_bytes=24 * MIB),
        cost_estimate=pl.CostEstimate(flops=1100000000, bytes_accessed=4 * MIB, transcendentals=0),
        name="first",
    )(*xs, w1, factors["t1"][0], factors["t1"][1])


def second_kernel(y, w2, out_ref):
    parts = []
    for odd in range(2):
        columns = pl.ds(256 * odd, 256)
        re = (y[0, :, columns], y[1, :, columns])
        im = (y[2, :, columns], y[3, :, columns])
        c = (w2[0, columns, :], w2[1, columns, :])
        s = (w2[2, columns, :], w2[3, columns, :])
        parts.append((dot3(re, c) + dot3(im, s), dot3(im, c) - dot3(re, s)))
    for k in range(2):
        even, odd = parts[0][k], parts[1][k]
        out_ref[k, :, pl.ds(0, 256)] = even + odd
        out_ref[k, :, pl.ds(256, 256)] = even - odd


def second(y, w2):
    return pl.pallas_call(
        second_kernel,
        out_shape=jax.ShapeDtypeStruct((2, 512, 512), f32),
        compiler_params=pltpu.CompilerParams(vmem_limit_bytes=24 * MIB),
        cost_estimate=pl.CostEstimate(flops=1600000000, bytes_accessed=5 * MIB, transcendentals=0),
        name="second",
    )(y, w2)


def inverse_kernel(shift_ref, spec, pa, pb, pc, pd, m3, w4, fine, coarse, out_ref, phases, zhi, zlo):
    slot = (lax.axis_index("z") * 4 + lax.axis_index("y")) * 2 + lax.axis_index("xh")
    series = jnp.where(slot < SERIES, slot, slot - SERIES)
    shift = shift_ref[series // 2]
    for p_in, dc, dx in ((pa, 0, 0), (pb, 0, 1), (pc, 1, 0), (pd, 1, 1)):
        place = partner(dc, dx)
        for u in range(2):
            for r in range(2):
                rows = pl.ds(pl.multiple_of(256 * u + 64 * place + 32 * r, 32), 32)
                phases[rows, :] = p_in[pl.ds(64 * r + 32 * u, 32), :]
    j = partner(0, 0)
    sign = jnp.where(j % 2 == 0, 1.0, -1.0)
    turn_re = jnp.where(j == 0, 1.0, jnp.where(j == 2, -1.0, 0.0))
    turn_im = jnp.where(j == 1, 1.0, jnp.where(j == 3, -1.0, 0.0))
    column = lax.broadcasted_iota(i32, (1, 512), 1)
    column_term = ((column * shift) & 511) * 512
    for block in range(512 // ROWS):
        rows = pl.ds(ROWS * block, ROWS)
        row = lax.broadcasted_iota(i32, (ROWS, 1), 0) + ROWS * block
        beta = row >> 5
        k1 = 256 * (row >> 8) + 8 * ((beta >> 2) & 1) + 2 * ((beta >> 1) & 1) + (beta & 1)
        k1 = k1 + 16 * ((row & 31) >> 1) + 4 * (row & 1)
        code = phases[rows, :].astype(i32) * 4 + k1 * shift + column_term
        sine, cosine = sin_cos(code)
        real, imag = spec[0, rows, :], spec[1, rows, :]
        ure = real * cosine - imag * sine
        uim = real * sine + imag * cosine
        are = ure[:, :128] + sign * ure[:, 256:384]
        aim = uim[:, :128] + sign * uim[:, 256:384]
        bre = ure[:, 128:256] + sign * ure[:, 384:]
        bim = uim[:, 128:256] + sign * uim[:, 384:]
        folded = jnp.concatenate(
            [are + turn_re * bre - turn_im * bim, aim + turn_re * bim + turn_im * bre], 1
        )
        mixed = dot3(split(folded), (m3[0], m3[1]))
        real, imag = mixed[:, :128], mixed[:, 128:]
        tcs, tss = [], []
        for b in range(ROWS // 32):
            at = pl.ds(block * (ROWS // 32) + b, 1)
            tc, ts = turned((fine[j, 0], fine[j, 1]), (coarse[j, 0, at, :], coarse[j, 1, at, :]))
            tcs.append(tc)
            tss.append(ts)
        tc, ts = jnp.concatenate(tcs, 0), jnp.concatenate(tss, 0)
        high, low = split(real * tc - imag * ts)
        zhi[rows, :128] = high
        zlo[rows, :128] = low
        high, low = split(real * ts + imag * tc)
        zhi[rows, 128:] = high
        zlo[rows, 128:] = low
    z = (zhi[...], zlo[...])
    by_cos = dot3((w4[0], w4[1]), z)
    by_sin = dot3((w4[2], w4[3]), z)
    real = by_cos[:, :128] - by_sin[:, 128:]
    imag = by_sin[:, :128] + by_cos[:, 128:]
    out_ref[...] = real * real + imag * imag


def inverse(shifts, spec, phases, m3, w4, factors):
    vmem = pl.BlockSpec(memory_space=pltpu.VMEM)
    return pl.pallas_call(
        inverse_kernel,
        out_shape=jax.ShapeDtypeStruct((256, 128), f32),
        in_specs=[pl.BlockSpec(memory_space=pltpu.SMEM)] + [vmem] * 9,
        scratch_shapes=[
            pltpu.VMEM((512, 512), jnp.int16),
            pltpu.VMEM((512, 256), bf16),
            pltpu.VMEM((512, 256), bf16),
        ],
        compiler_params=pltpu.CompilerParams(vmem_limit_bytes=24 * MIB),
        cost_estimate=pl.CostEstimate(flops=800000000, bytes_accessed=4 * MIB, transcendentals=0),
        name="inverse",
    )(shifts, spec, *phases, m3, w4, factors["t3"][0], factors["t3"][1])


def combine_kernel(power_ref, weight_ref, order_ref, out_ref):
    rows = []
    for g in range(GROUPS):
        total = jnp.sum((weight_ref[g] * power_ref[...]).reshape(32, 8, 128), axis=0)
        places = [total[4 * c + x : 4 * c + x + 1] + total[4 * c + x + 2 : 4 * c + x + 3] for c in range(2) for x in range(2)]
        rows.append(jnp.concatenate(places, 1))
    total = jnp.concatenate(rows, 0)
    high = total.astype(bf16).astype(f32)
    rest = total - high
    middle = rest.astype(bf16).astype(f32)
    pieces = jnp.concatenate([high, middle, rest - middle, jnp.zeros_like(high)], 0).astype(bf16)
    ordered = dot(pieces, order_ref[...])
    out_ref[...] = ordered[0:4] + ordered[4:8] + ordered[8:12]


def combine(power, weight, order):
    return pl.pallas_call(
        combine_kernel,
        out_shape=jax.ShapeDtypeStruct((GROUPS, 512), f32),
        compiler_params=pltpu.CompilerParams(vmem_limit_bytes=8 * MIB),
        name="combine",
    )(power, weight, order)


def on_device(voltages, chirp_phase, intersection, group_of):
    factors = jax.tree.map(jnp.asarray, table_factors())
    w1, w2, w4, m3, weight, order = tables(group_of, factors)
    got = lax.all_to_all(pack(voltages, chirp_phase), SPREAD, 0, 0, tiled=True)
    own_x = samples(got)
    xb = lax.ppermute(own_x, "xl", SWAP)
    xc = lax.ppermute(own_x, "core", SWAP)
    own_p = phases(got)
    xb, own_p, w1, w2, w4, m3 = lax.optimization_barrier((xb, own_p, w1, w2, w4, m3))
    xd = lax.ppermute(xb, "core", SWAP)
    pb = lax.ppermute(own_p, "xl", SWAP)
    pc = lax.ppermute(own_p, "core", SWAP)
    y = first((own_x, xb, xc, xd), w1, factors)
    y, pb = lax.optimization_barrier((y, pb))
    pd = lax.ppermute(pb, "core", SWAP)
    spec = second(y, w2)
    power = inverse(intersection, spec, (own_p, pb, pc, pd), m3, w4, factors)
    spread = lax.all_to_all(power.reshape(256, 1, 128), AXES, 0, 0, tiled=True)
    return combine(spread.reshape(256, 128), weight, order).reshape(1, GROUPS, 512)


def solution(mesh):
    inner = Mesh(mesh.devices.reshape(8, 4, 2, 2, 2), AXES)
    in_specs = (P(None, None, None, None, AXES), P(None, ("z", "y", "core"), None), P(), P())
    return jax.shard_map(
        on_device, mesh=inner, in_specs=in_specs, out_specs=P(None, None, AXES), check_vma=False
    )
```

```python
import functools
import math

import jax
import jax.numpy as jnp
import numpy as np
from jax import lax
from jax.experimental import pallas as pl
from jax.experimental.pallas import tpu as pltpu
from jax.sharding import Mesh
from jax.sharding import PartitionSpec as P

NFFT = 262144
F1 = 512
F2 = 512
CHANS = 24
POLS = 2
SERIES = CHANS * POLS
SLOTS = 64
GROUPS = 4
AXES = ("z", "y", "core", "xh", "xl")
SPREAD = ("z", "y", "xh")
SWAP = [(0, 1), (1, 0)]
MIB = 1 << 20
CHUNK = 24

f32 = jnp.float32
bf16 = jnp.bfloat16
i32 = jnp.int32


def cos_sin(index, period):
    angle = 2.0 * np.pi * (index % period) / period
    return np.stack([np.cos(angle), np.sin(angle)]).astype(np.float32)


@functools.cache
def table_factors():
    beta = np.arange(8)
    m = np.arange(64)
    fine = 16 * (m // 2) + 4 * (m % 2)
    coarse = 8 * (beta // 4) + 2 * (beta // 2 % 2) + beta % 2
    place = coarse.reshape(4, 2)
    sample_row = np.concatenate([(place[:, jj, None] + fine[None, :]).reshape(-1) for jj in range(2)])
    low = fine[:32]
    high_part = np.concatenate([coarse, 256 + coarse])
    k1 = (high_part[:, None] + low[None, :]).reshape(-1)
    half = np.arange(256)
    sample_column = np.concatenate([2 * half, 2 * half + 1])
    quarter = np.arange(128)
    out_column = 4 * quarter[None, :] + np.arange(4)[:, None]

    def outer(rows, columns, period):
        return cos_sin(rows[:, None] * columns[None, :], period)

    def outers(rows, columns, period):
        return np.stack([outer(rows, c, period) for c in columns])

    even_odd = np.concatenate([128 * np.arange(4), 128 * np.arange(4) + 1])
    return dict(
        w1=(outer(low, sample_row, F1), outer(coarse, sample_row, F1)),
        w2=(outer(2 * m, half, F2), outer(even_odd, half, F2)),
        w4=(outer(m, k1, F1), outer(64 * np.arange(4), k1, F1)),
        m3=outers(quarter, out_column, F2),
        t1=(outer(low, sample_column, NFFT), outer(high_part, sample_column, NFFT)),
        t3=(outers(low, out_column, NFFT), outers(high_part, out_column, NFFT)),
    )


def split(value):
    high = value.astype(bf16)
    return high, (value - high.astype(f32)).astype(bf16)


def turned(fine, coarse):
    return fine[0] * coarse[0] - fine[1] * coarse[1], fine[1] * coarse[0] + fine[0] * coarse[1]


def encode(phase):
    steps = jnp.round(phase * (16384.0 / math.pi))
    size = jnp.abs(steps).astype(i32)
    value = (1.0 + (size & 127).astype(f32) * (1.0 / 128.0)) * 2.0**-64
    for k in range(7):
        value = jnp.where(((size >> (7 + k)) & 1) == 1, value * 2.0 ** (1 << k), value)
    return jnp.where(steps < 0.0, -value, value)


def decode(coded):
    value = jnp.abs(coded) * 2.0**64
    size = jnp.zeros_like(value)
    for k in reversed(range(7)):
        large = value >= 2.0 ** (1 << k)
        value = jnp.where(large, value * 2.0 ** -(1 << k), value)
        size = jnp.where(large, size + 256.0 * (1 << k), size)
    size = size + (value - 1.0) * 256.0
    return jnp.where(coded < 0.0, -size, size).astype(i32)


def pack_kernel(v_hbm, c_hbm, out_ref, v_ref, c_ref, wide, narrow, tall, v_sem, c_sem):
    v_copy = pltpu.make_async_copy(v_hbm, v_ref, v_sem)
    c_copy = pltpu.make_async_copy(c_hbm, c_ref, c_sem)
    v_copy.start()
    c_copy.start()
    x_pos = 2 * lax.axis_index("xh") + lax.axis_index("xl")
    into = lax.broadcasted_iota(i32, (256, 256), 1)
    sample = lax.broadcasted_iota(i32, (256, 256), 0)
    pick = (sample == 2 * (into & 127) + (into >> 7)).astype(f32).astype(bf16)
    v_copy.wait()
    samples = v_ref[...].reshape(SERIES * 2, 1024)
    for jj in range(2):
        for u in range(2):
            start = 512 * jj + 256 * u
            piece = jnp.dot(samples[:, start : start + 256], pick, preferred_element_type=f32)
            for odd in range(2):
                i = 4 * jj + 2 * odd + u
                wide[pl.ds(SERIES * 2 * i, SERIES * 2), :] = piece[:, 128 * odd : 128 * odd + 128]
    for reim in range(2):
        for i in range(8):
            rows = wide[pl.ds(SERIES * 2 * i + reim, SERIES, stride=2), :]
            tall[pl.ds(reim * 8 + i, SERIES, stride=CHUNK), :] = rows
    c_copy.wait()
    for kk in range(4):
        narrow[pl.ds(CHANS * 8 * kk, CHANS * 8), :] = c_ref[:, pl.ds(128 * kk, 128)]
    for r in range(2):
        for kk in range(4):
            phase = narrow[pl.ds(CHANS * 8 * kk + 2 * x_pos + r, CHANS, stride=8), :]
            coded = encode(phase)
            for pol in range(2):
                base = pol * CHUNK + 16 + r * 4 + kk
                tall[pl.ds(base, CHANS, stride=2 * CHUNK), :] = coded
    packed = tall[...].astype(bf16).reshape(SERIES, CHUNK, 128)
    out_ref[pl.ds(0, SERIES)] = packed
    out_ref[pl.ds(SERIES, SLOTS - SERIES)] = packed[: SLOTS - SERIES]


def pack(voltages, chirp):
    return pl.pallas_call(
        pack_kernel,
        out_shape=jax.ShapeDtypeStruct((SLOTS, CHUNK, 128), bf16),
        in_specs=[pl.BlockSpec(memory_space=pltpu.HBM)] * 2,
        scratch_shapes=[
            pltpu.VMEM((CHANS, POLS, 2, 1024), bf16),
            pltpu.VMEM((CHANS * 8, 512), f32),
            pltpu.VMEM((SERIES * 16, 128), f32),
            pltpu.VMEM((CHANS * 32, 128), f32),
            pltpu.VMEM((SERIES * CHUNK, 128), f32),
            pltpu.SemaphoreType.DMA,
            pltpu.SemaphoreType.DMA,
        ],
        compiler_params=pltpu.CompilerParams(vmem_limit_bytes=16 * MIB),
        name="pack",
    )(voltages.reshape(CHANS, POLS, 2, 1024), chirp.reshape(CHANS * 8, 512))


def samples_kernel(got_ref, x_ref, tall):
    tall[...] = got_ref[:, pl.ds(0, 16), :].astype(f32).reshape(SLOTS * 16, 128)
    for reim in range(2):
        for i in range(8):
            rows = tall[pl.ds(reim * 8 + i, SLOTS, stride=16), :]
            x_ref[reim, pl.ds(64 * (i // 4), 64), pl.ds(128 * (i % 4), 128)] = rows.astype(bf16)


def samples(got):
    return pl.pallas_call(
        samples_kernel,
        out_shape=jax.ShapeDtypeStruct((2, 128, 512), bf16),
        scratch_shapes=[pltpu.VMEM((SLOTS * 16, 128), f32)],
        compiler_params=pltpu.CompilerParams(vmem_limit_bytes=16 * MIB),
        name="samples",
    )(got)


def phases_kernel(got_ref, phase_ref, tall):
    tall[...] = got_ref[:, pl.ds(16, 8), :].astype(f32).reshape(SLOTS * 8, 128)
    for r in range(2):
        for kk in range(4):
            coded = tall[pl.ds(r * 4 + kk, SLOTS, stride=8), :]
            phase_ref[pl.ds(64 * r, 64), pl.ds(128 * kk, 128)] = decode(coded).astype(jnp.int16)


def phases(got):
    return pl.pallas_call(
        phases_kernel,
        out_shape=jax.ShapeDtypeStruct((128, 512), jnp.int16),
        scratch_shapes=[pltpu.VMEM((SLOTS * 8, 128), f32)],
        compiler_params=pltpu.CompilerParams(vmem_limit_bytes=16 * MIB),
        cost_estimate=pl.CostEstimate(flops=3000000, bytes_accessed=MIB, transcendentals=0),
        name="phases",
    )(got)


def partner(relative):
    return relative ^ (2 * lax.axis_index("core") + lax.axis_index("xl"))


def tables_kernel(group_ref, f1, c1, f2, c2, f4, c4, m3, w1_ref, w2_ref, w4_ref, m3_ref, weight_ref, order_ref):
    for fine, coarse, out, height, blocks, mask in (
        (f1, c1, w1_ref, 32, 8, 2 * partner(0)),
        (f2, c2, w2_ref, 64, 8, 0),
        (f4, c4, w4_ref, 64, 4, 0),
    ):

        def block(beta, carry, fine=fine, coarse=coarse, out=out, height=height, mask=mask):
            row = pl.ds(beta ^ mask, 1)
            rows = pl.ds(pl.multiple_of(height * beta, height), height)
            values = turned((fine[0], fine[1]), (coarse[0, row, :], coarse[1, row, :]))
            for kind, value in enumerate(values):
                high, low = split(value)
                out[2 * kind, rows, :] = high
                out[2 * kind + 1, rows, :] = low
            return carry

        lax.fori_loop(0, blocks, block, 0)
    j = partner(0)
    cosine, sine = m3[j, 0], m3[j, 1]
    for row, column, value in ((0, 0, cosine), (0, 1, sine), (1, 0, -sine), (1, 1, cosine)):
        high, low = split(value)
        m3_ref[0, pl.ds(128 * row, 128), pl.ds(128 * column, 128)] = high
        m3_ref[1, pl.ds(128 * row, 128), pl.ds(128 * column, 128)] = low
    source = lax.broadcasted_iota(i32, (256, 128), 0)
    channel = (source // 8 * 2 + source // 2 % 2) // 2
    owner = jnp.zeros((256, 128), i32) - 1
    counts = [jnp.int32(0)] * GROUPS
    for c in range(CHANS):
        g = group_ref[c]
        owner = jnp.where(channel == c, g, owner)
        counts = [n + (g == k).astype(i32) for k, n in enumerate(counts)]
    for k in range(GROUPS):
        count = jnp.broadcast_to(counts[k], (256, 128)).astype(f32)
        scale = 1.0 / (2.0 * count) * (1.0 / NFFT) * (1.0 / NFFT)
        weight_ref[k] = jnp.where(owner == k, scale, 0.0)
    source = lax.broadcasted_iota(i32, (512, 512), 0)
    column = lax.broadcasted_iota(i32, (512, 512), 1)
    order_ref[...] = (column == 4 * (source & 127) + (source >> 7)).astype(f32).astype(bf16)


def tables(group_of, factors):
    vmem = pl.BlockSpec(memory_space=pltpu.VMEM)
    flat = [factors["w1"][0], factors["w1"][1], factors["w2"][0], factors["w2"][1]]
    flat += [factors["w4"][0], factors["w4"][1], factors["m3"]]
    return pl.pallas_call(
        tables_kernel,
        out_shape=(
            jax.ShapeDtypeStruct((4, 256, 512), bf16),
            jax.ShapeDtypeStruct((4, 512, 256), bf16),
            jax.ShapeDtypeStruct((4, 256, 512), bf16),
            jax.ShapeDtypeStruct((2, 256, 256), bf16),
            jax.ShapeDtypeStruct((GROUPS, 256, 128), f32),
            jax.ShapeDtypeStruct((512, 512), bf16),
        ),
        in_specs=[pl.BlockSpec(memory_space=pltpu.SMEM)] + [vmem] * 7,
        compiler_params=pltpu.CompilerParams(vmem_limit_bytes=16 * MIB),
        cost_estimate=pl.CostEstimate(flops=8000000, bytes_accessed=6 * MIB, transcendentals=0),
        name="tables",
    )(group_of, *flat)


def dot(a, b):
    return jnp.dot(a, b, preferred_element_type=f32)


def dot3(a, b):
    return dot(a[0], b[0]) + dot(a[0], b[1]) + dot(a[1], b[0])


def sin_cos(code):
    quadrant = (code + 32768) >> 16
    rest = (code - (quadrant << 16)).astype(f32) * (2.0 * math.pi / NFFT)
    sq = rest * rest
    sine = rest + rest * sq * (
        -1.6666654611e-1 + sq * (8.3321608736e-3 + sq * -1.9515295891e-4)
    )
    cosine = 1.0 + sq * (
        -0.5 + sq * (4.166664568298827e-2 + sq * (-1.388731625493765e-3 + sq * 2.443315711809948e-5))
    )
    odd = (quadrant & 1) == 1
    sin_out = jnp.where(odd, cosine, sine)
    cos_out = jnp.where(odd, sine, cosine)
    sin_out = jnp.where((quadrant & 2) == 2, -sin_out, sin_out)
    cos_out = jnp.where(((quadrant + 1) & 2) == 2, -cos_out, cos_out)
    return sin_out, cos_out


def first_kernel(xa, xb, xc, xd, w1, fine, coarse, y_ref, xre, xim):
    for relative, x_in in enumerate((xa, xb, xc, xd)):
        place = partner(relative)
        for jj in range(2):
            rows = pl.ds(pl.multiple_of(jj * 256 + place * 64, 64), 64)
            xre[rows, :] = x_in[0, pl.ds(64 * jj, 64), :]
            xim[rows, :] = x_in[1, pl.ds(64 * jj, 64), :]
    for block in range(2):
        parts = []
        for jj in range(2):
            rows, columns = pl.ds(128 * block, 128), pl.ds(256 * jj, 256)
            c0, c1, s0, s1 = (w1[k, rows, columns] for k in range(4))
            re, im = xre[columns, :], xim[columns, :]
            real = dot(c0, re) + dot(c1, re) + dot(s0, im) + dot(s1, im)
            imag = dot(c0, im) + dot(c1, im) - (dot(s0, re) + dot(s1, re))
            parts.append((real, imag))
        (even_re, even_im), (odd_re, odd_im) = parts
        for u, (real, imag) in enumerate(
            ((even_re + odd_re, even_im + odd_im), (even_re - odd_re, even_im - odd_im))
        ):
            tcs, tss = [], []
            for beta in range(4):
                row = pl.ds(8 * u + ((4 * block + beta) ^ (2 * partner(0))), 1)
                tc, ts = turned((fine[0], fine[1]), (coarse[0, row, :], coarse[1, row, :]))
                tcs.append(tc)
                tss.append(ts)
            tc, ts = jnp.concatenate(tcs, 0), jnp.concatenate(tss, 0)
            rows = pl.ds(256 * u + 128 * block, 128)
            y_ref[0, rows, :], y_ref[1, rows, :] = split(real * tc + imag * ts)
            y_ref[2, rows, :], y_ref[3, rows, :] = split(imag * tc - real * ts)


def first(xs, w1, factors):
    return pl.pallas_call(
        first_kernel,
        out_shape=jax.ShapeDtypeStruct((4, 512, 512), bf16),
        scratch_shapes=[pltpu.VMEM((512, 512), bf16), pltpu.VMEM((512, 512), bf16)],
        compiler_params=pltpu.CompilerParams(vmem_limit_bytes=24 * MIB),
        cost_estimate=pl.CostEstimate(flops=1100000000, bytes_accessed=4 * MIB, transcendentals=0),
        name="first",
    )(*xs, w1, factors["t1"][0], factors["t1"][1])


def second_kernel(y, w2, out_ref):
    parts = []
    for odd in range(2):
        columns = pl.ds(256 * odd, 256)
        re = (y[0, :, columns], y[1, :, columns])
        im = (y[2, :, columns], y[3, :, columns])
        c = (w2[0, columns, :], w2[1, columns, :])
        s = (w2[2, columns, :], w2[3, columns, :])
        parts.append((dot3(re, c) + dot3(im, s), dot3(im, c) - dot3(re, s)))
    for k in range(2):
        even, odd = parts[0][k], parts[1][k]
        out_ref[k, :, pl.ds(0, 256)] = even + odd
        out_ref[k, :, pl.ds(256, 256)] = even - odd


def second(y, w2):
    return pl.pallas_call(
        second_kernel,
        out_shape=jax.ShapeDtypeStruct((2, 512, 512), f32),
        compiler_params=pltpu.CompilerParams(vmem_limit_bytes=24 * MIB),
        cost_estimate=pl.CostEstimate(flops=1600000000, bytes_accessed=5 * MIB, transcendentals=0),
        name="second",
    )(y, w2)


def shard_inverse(relative, phase_ref, spec, m3, fine, coarse, shift):
    j = partner(0)
    place = partner(relative)
    sign = jnp.where(j % 2 == 0, 1.0, -1.0)
    turn_re = jnp.where(j == 0, 1.0, jnp.where(j == 2, -1.0, 0.0))
    turn_im = jnp.where(j == 1, 1.0, jnp.where(j == 3, -1.0, 0.0))
    column = lax.broadcasted_iota(i32, (1, 512), 1)
    column_term = ((column * shift) & 511) * 512
    row = lax.broadcasted_iota(i32, (128, 1), 0)
    k1 = 256 * (row >> 6) + 8 * (place >> 1) + 2 * (place & 1) + ((row >> 5) & 1)
    k1 = k1 + 16 * ((row & 31) >> 1) + 4 * (row & 1)
    phase = jnp.concatenate([phase_ref[pl.ds(64 * r + 32 * u, 32), :] for u in range(2) for r in range(2)], 0)
    code = phase.astype(i32) * 4 + k1 * shift + column_term
    sine, cosine = sin_cos(code)
    real, imag = (
        jnp.concatenate([spec[k, pl.ds(256 * u + 64 * relative, 64), :] for u in range(2)], 0) for k in range(2)
    )
    ure = real * cosine - imag * sine
    uim = real * sine + imag * cosine
    are = ure[:, :128] + sign * ure[:, 256:384]
    aim = uim[:, :128] + sign * uim[:, 256:384]
    bre = ure[:, 128:256] + sign * ure[:, 384:]
    bim = uim[:, 128:256] + sign * uim[:, 384:]
    folded = jnp.concatenate([are + turn_re * bre - turn_im * bim, aim + turn_re * bim + turn_im * bre], 1)
    mixed = dot3(split(folded), (m3[0], m3[1]))
    real, imag = mixed[:, :128], mixed[:, 128:]
    tcs, tss = [], []
    for u in range(2):
        for r in range(2):
            at = pl.ds(8 * u + 2 * place + r, 1)
            tc, ts = turned((fine[j, 0], fine[j, 1]), (coarse[j, 0, at, :], coarse[j, 1, at, :]))
            tcs.append(tc)
            tss.append(ts)
    tc, ts = jnp.concatenate(tcs, 0), jnp.concatenate(tss, 0)
    return split(jnp.concatenate([real * tc - imag * ts, real * ts + imag * tc], 1))


def own_shift(shift_ref):
    slot = (lax.axis_index("z") * 4 + lax.axis_index("y")) * 2 + lax.axis_index("xh")
    series = jnp.where(slot < SERIES, slot, slot - SERIES)
    return shift_ref[series // 2]


def early_kernel(shift_ref, spec, pa, pb, pc, m3, fine, coarse, z_ref):
    shift = own_shift(shift_ref)
    for relative, phase_ref in enumerate((pa, pb, pc)):
        rows = pl.ds(128 * relative, 128)
        z_ref[0, rows, :], z_ref[1, rows, :] = shard_inverse(relative, phase_ref, spec, m3, fine, coarse, shift)


def early(shifts, spec, phases, m3, factors):
    vmem = pl.BlockSpec(memory_space=pltpu.VMEM)
    return pl.pallas_call(
        early_kernel,
        out_shape=jax.ShapeDtypeStruct((2, 384, 256), bf16),
        in_specs=[pl.BlockSpec(memory_space=pltpu.SMEM)] + [vmem] * 7,
        compiler_params=pltpu.CompilerParams(vmem_limit_bytes=24 * MIB),
        cost_estimate=pl.CostEstimate(flops=400000000, bytes_accessed=3 * MIB, transcendentals=0),
        name="early",
    )(shifts, spec, *phases, m3, factors["t3"][0], factors["t3"][1])


def late_kernel(shift_ref, spec, z_ref, pd, m3, fine, coarse, w4, out_ref, zhi, zlo):
    z_last = shard_inverse(3, pd, spec, m3, fine, coarse, own_shift(shift_ref))
    for relative in range(4):
        for u in range(2):
            rows = pl.ds(pl.multiple_of(256 * u + 64 * partner(relative), 64), 64)
            half = pl.ds(128 * relative + 64 * u, 64)
            for k, z_out in enumerate((zhi, zlo)):
                z_out[rows, :] = z_ref[k, half, :] if relative < 3 else z_last[k][64 * u : 64 * u + 64]
    z = (zhi[...], zlo[...])
    by_cos = dot3((w4[0], w4[1]), z)
    by_sin = dot3((w4[2], w4[3]), z)
    real = by_cos[:, :128] - by_sin[:, 128:]
    imag = by_sin[:, :128] + by_cos[:, 128:]
    out_ref[...] = real * real + imag * imag


def late(shifts, spec, z, pd, m3, w4, factors):
    vmem = pl.BlockSpec(memory_space=pltpu.VMEM)
    return pl.pallas_call(
        late_kernel,
        out_shape=jax.ShapeDtypeStruct((256, 128), f32),
        in_specs=[pl.BlockSpec(memory_space=pltpu.SMEM)] + [vmem] * 7,
        scratch_shapes=[pltpu.VMEM((512, 256), bf16), pltpu.VMEM((512, 256), bf16)],
        compiler_params=pltpu.CompilerParams(vmem_limit_bytes=24 * MIB),
        cost_estimate=pl.CostEstimate(flops=500000000, bytes_accessed=2 * MIB, transcendentals=0),
        name="late",
    )(shifts, spec, z, pd, m3, factors["t3"][0], factors["t3"][1], w4)


def combine_kernel(power_ref, weight_ref, order_ref, out_ref):
    rows = []
    for g in range(GROUPS):
        total = jnp.sum((weight_ref[g] * power_ref[...]).reshape(32, 8, 128), axis=0)
        places = [total[4 * c + x : 4 * c + x + 1] + total[4 * c + x + 2 : 4 * c + x + 3] for c in range(2) for x in range(2)]
        rows.append(jnp.concatenate(places, 1))
    total = jnp.concatenate(rows, 0)
    high = total.astype(bf16).astype(f32)
    rest = total - high
    middle = rest.astype(bf16).astype(f32)
    pieces = jnp.concatenate([high, middle, rest - middle, jnp.zeros_like(high)], 0).astype(bf16)
    ordered = dot(pieces, order_ref[...])
    out_ref[...] = ordered[0:4] + ordered[4:8] + ordered[8:12]


def combine(power, weight, order):
    return pl.pallas_call(
        combine_kernel,
        out_shape=jax.ShapeDtypeStruct((GROUPS, 512), f32),
        compiler_params=pltpu.CompilerParams(vmem_limit_bytes=8 * MIB),
        name="combine",
    )(power, weight, order)


def on_device(voltages, chirp_phase, intersection, group_of):
    factors = jax.tree.map(jnp.asarray, table_factors())
    w1, w2, w4, m3, weight, order = tables(group_of, factors)
    got = lax.all_to_all(pack(voltages, chirp_phase), SPREAD, 0, 0, tiled=True)
    own_x = samples(got)
    xb = lax.ppermute(own_x, "xl", SWAP)
    xc = lax.ppermute(own_x, "core", SWAP)
    own_p = phases(got)
    xb, own_p, w1, w2, w4, m3 = lax.optimization_barrier((xb, own_p, w1, w2, w4, m3))
    xd = lax.ppermute(xb, "core", SWAP)
    pb = lax.ppermute(own_p, "xl", SWAP)
    pc = lax.ppermute(own_p, "core", SWAP)
    y = first((own_x, xb, xc, xd), w1, factors)
    spec = second(y, w2)
    spec, pb = lax.optimization_barrier((spec, pb))
    pd = lax.ppermute(pb, "core", SWAP)
    z = early(intersection, spec, (own_p, pb, pc), m3, factors)
    power = late(intersection, spec, z, pd, m3, w4, factors)
    spread = lax.all_to_all(power.reshape(256, 1, 128), AXES, 0, 0, tiled=True)
    return combine(spread.reshape(256, 128), weight, order).reshape(1, GROUPS, 512)


def solution(mesh):
    inner = Mesh(mesh.devices.reshape(8, 4, 2, 2, 2), AXES)
    in_specs = (P(None, None, None, None, AXES), P(None, ("z", "y", "core"), None), P(), P())
    return jax.shard_map(
        on_device, mesh=inner, in_specs=in_specs, out_specs=P(None, None, AXES), check_vma=False
    )
```
